768 devices in a mesh: section: 32 (over y, x_lo, core), depth: 2 (over x_hi), res: 12 (over z).
Axes of the slice: x: 4 (x_hi: 2, x_lo: 2; x = x_hi * 2 + x_lo), y: 8, z: 12, core: 2. Of those that a mesh axis runs over, the one named last changes fastest.
Arguments:
- slab: bfloat16 [32, 48, 96, 768], P('section', ('depth', 'res')), may hold values from -6 to 6
- tokens: int32 [48, 96], P(('depth', 'res')), may hold values from 0 to 32
- lengths: int32 [32, 48], P('section'), may hold values from 24 to 96, as said below
- embed: bfloat16 [33, 768], replicated, may hold values from -6 to 6
- row_qkv: bfloat16 [32, 768, 2304], P('section'), may hold values from -1 to 1
- row_out: bfloat16 [32, 768, 768], P('section'), may hold values from -0.21875 to 0.21875
- col_qkv: bfloat16 [32, 768, 2304], P('section'), may hold values from -1 to 1
- col_out: bfloat16 [32, 768, 768], P('section'), may hold values from -0.21875 to 0.21875
Outputs:
- next_slab: bfloat16 [32, 48, 96, 768], P('section', ('depth', 'res'))
The draws below stay inside these ranges and needn't reach their ends.
Inputs may be any that keep to these rules, and one draw needn't show every extreme that they name: `lengths`: row 0 of every section's micro-batch has length 96.
All inputs are finite; a program needn't handle non-finite values.
Results may differ from the reference program's by a relative error of at most 0.012.
Values may be sent and summed in bfloat16 or wider, within the bound.
No kernel may reach another device: no remote copies, remote signals or barrier semaphores. Data moves between devices by JAX's collectives and lax.ppermute only.
A program may use at most 64 MiB of HBM per device.

```python
import math
import jax
import jax.numpy as jnp
from jax import lax

D = 768
H = 12
HD = 64
VOCAB = 33
L = 96
ROWS = 48
N_SECTION = 32


def draw_lengths(key, part):
    drawn = jax.random.randint(key, (N_SECTION, ROWS), L // 4, L + 1)
    row_index = jnp.arange(ROWS, dtype=jnp.int32)[None, :]
    return jnp.where(row_index == 0, L, drawn).astype(jnp.int32)


def draw_slab(key, part):
    shape = (N_SECTION, ROWS, L, D)
    first = jax.random.fold_in(jax.random.fold_in(key, 11), 0)
    values = jax.random.normal(first, shape, jnp.float32)
    return jnp.clip(values, -6.0, 6.0).astype(jnp.bfloat16)


def projection_draw(key, salt):
    shape = (N_SECTION, D, 3 * D)
    inner = jax.random.fold_in(key, salt)
    spread = D ** (-0.5)
    values = jnp.clip(jax.random.normal(inner, shape, jnp.float32), -4.0, 4.0) * spread
    return values.astype(jnp.bfloat16)


def draw_row_qkv(key, part):
    return projection_draw(key, 23)


def draw_col_qkv(key, part):
    return projection_draw(key, 37)


def set_ends(array, own_key, smallest, largest):
    longest = array.shape.index(max(array.shape))
    spots = []
    for shift in (0, 1):
        where = [jax.random.randint(jax.random.fold_in(own_key, axis), (), 0, length) for axis, length in enumerate(array.shape)]
        where[longest] = (where[longest] + shift) % array.shape[longest]
        spots.append(tuple(where))
    return array.at[spots[0]].set(smallest).at[spots[1]].set(largest)


def shard_levels(key, extent, cuts, low, high):
    level = 1.0
    for position, shards_of in cuts:
        draws = jax.random.uniform(jax.random.fold_in(jax.random.fold_in(key, 6), position), (shards_of,), jnp.float32, low / len(cuts), high / len(cuts))
        level = level * jnp.repeat(jnp.exp(draws), extent[position] // shards_of).reshape((-1,) + (1,) * (len(extent) - 1 - position))
    return level


def bell_draw(stream_key, shape, deviation, most, cuts=(), kind=jnp.bfloat16):
    entries = jax.random.normal(stream_key, shape, jnp.float32) * deviation
    if len(cuts) > 0:
        entries = shard_levels(stream_key, shape, cuts, -0.22, 0.18) * entries
    return jnp.clip(entries, min=-most, max=most).astype(kind)


def setup_inputs(seed: int = 0) -> dict:
    arg_keys = jax.random.split(jax.random.key(seed), 9)
    slab = draw_slab(jax.random.fold_in(arg_keys[8], 71), 0)
    tokens = set_ends(jax.random.randint(arg_keys[1], (ROWS, L), 0, VOCAB), jax.random.fold_in(arg_keys[1], 1), 0, VOCAB - 1).astype(jnp.int32)
    lengths = draw_lengths(jax.random.fold_in(arg_keys[8], 71), 0)
    embed = bell_draw(arg_keys[3], (VOCAB, D), 1.0, 6.0)
    row_qkv = draw_row_qkv(jax.random.fold_in(arg_keys[8], 71), 0)
    row_out = bell_draw(arg_keys[5], (N_SECTION, D, D), D ** -0.5, 0.21875, ((0, 32),))
    col_qkv = draw_col_qkv(jax.random.fold_in(arg_keys[8], 71), 0)
    col_out = bell_draw(arg_keys[7], (N_SECTION, D, D), D ** -0.5, 0.21875, ((0, 32),))
    return dict(slab=slab, tokens=tokens, lengths=lengths, embed=embed, row_qkv=row_qkv, row_out=row_out, col_qkv=col_qkv, col_out=col_out)


def normalize(values):
    values = values.astype(jnp.float32)
    center = lax.optimization_barrier(jnp.mean(values, axis=-1, keepdims=True))
    spread = lax.optimization_barrier(jnp.mean((values - center) ** 2, axis=-1, keepdims=True))
    return (values - center) * lax.rsqrt(spread + 1e-05)

def section_layer(operands):
    slab_rows, row_lens, w_rowqkv, w_rowout, w_colqkv, w_colout = operands
    rows_all, length, width = slab_rows.shape
    positions = jnp.arange(length, dtype=jnp.int32)
    keep_mask = positions[None, :] < row_lens[:, None]
    normed = normalize(slab_rows).astype(jnp.bfloat16)
    packed = jnp.dot(normed.reshape(-1, width), w_rowqkv, preferred_element_type=jnp.float32).astype(jnp.bfloat16)
    packed = packed.reshape(rows_all, length, 3, H, HD)
    queries = packed[:, :, 0].astype(jnp.float32)
    key_rows = packed[:, :, 1]
    key_rows = jnp.where(keep_mask[:, :, None, None], key_rows, jnp.zeros_like(key_rows)).astype(jnp.float32)
    value_rows = packed[:, :, 2].astype(jnp.float32)
    tied = jnp.einsum('rihe,rjhe->hij', queries, key_rows) / math.sqrt(HD * rows_all)
    scores = jnp.where(keep_mask[:, None, None, :], tied[None], -1e+30)
    weights = jax.nn.softmax(scores, axis=-1).astype(jnp.bfloat16).astype(jnp.float32)
    mixed = jnp.einsum('rhij,rjhe->rihe', weights, value_rows).astype(jnp.bfloat16).reshape(-1, width)
    after_row = (slab_rows.astype(jnp.float32) + jnp.dot(mixed, w_rowout, preferred_element_type=jnp.float32).reshape(slab_rows.shape)).astype(jnp.bfloat16)
    normed_col = normalize(after_row).astype(jnp.bfloat16)
    packed_col = jnp.dot(normed_col.reshape(-1, width), w_colqkv, preferred_element_type=jnp.float32).astype(jnp.bfloat16)
    packed_col = packed_col.reshape(rows_all, length, 3, H, HD).astype(jnp.float32)
    col_scores = jnp.einsum('rihe,sihe->ihrs', packed_col[:, :, 0], packed_col[:, :, 1]) / math.sqrt(HD)
    col_scores = jnp.where(keep_mask.T[:, None, None, :], col_scores, -1e+30)
    col_weights = jax.nn.softmax(col_scores, axis=-1).astype(jnp.bfloat16).astype(jnp.float32)
    col_mixed = jnp.einsum('ihrs,sihe->rihe', col_weights, packed_col[:, :, 2]).astype(jnp.bfloat16).reshape(-1, width)
    result = after_row.astype(jnp.float32) + jnp.dot(col_mixed, w_colout, preferred_element_type=jnp.float32).reshape(slab_rows.shape)
    return result.astype(jnp.bfloat16)

def reference(slab, tokens, lengths, embed, row_qkv, row_out, col_qkv, col_out):
    layered = lax.map(section_layer, (slab[:-1], lengths[:-1], row_qkv[:-1], row_out[:-1], col_qkv[:-1], col_out[:-1]))
    entering = embed[tokens]
    return jnp.concatenate([entering[None], layered], axis=0)
```

```python
import functools
import math

import jax
import jax.numpy as jnp
from jax import lax
from jax.experimental import pallas as pl
from jax.experimental.pallas import tpu as pltpu
from jax.sharding import PartitionSpec as P

H = 12
HD = 64
GROUP = ("depth", "res")
SHORTEST = 24
NEG = -1e30
F32 = jnp.float32
BF16 = jnp.bfloat16


def iota(shape, dim):
    return lax.broadcasted_iota(jnp.int32, shape, dim)


def dot(a, b):
    return jnp.dot(a, b, preferred_element_type=F32)


def dot_t(a, b):
    return lax.dot_general(a, b, (((1,), (1,)), ((), ())), preferred_element_type=F32)


def normalize(values):
    values = values.astype(F32)
    center = jnp.mean(values, axis=-1, keepdims=True)
    off = values - center
    spread = jnp.mean(off * off, axis=-1, keepdims=True)
    return (off * lax.rsqrt(spread + 1e-05)).astype(BF16)


def row_length(lens, row):
    return jnp.sum(jnp.where(iota(lens.shape, 1) == row, lens, 0), axis=1, keepdims=True)


def place_of():
    return lax.axis_index(GROUP)


def two_heads(tile):
    first = iota(tile.shape, 1) < HD
    none = jnp.zeros_like(tile)
    return jnp.concatenate([jnp.where(first, tile, none), jnp.where(first, none, tile)], axis=0)


def pick_heads(both):
    n = both.shape[0] // 2
    return jnp.where(iota((n, 2 * HD), 1) < HD, both[:n], both[n:])


def soft(scores):
    top = jnp.max(scores, axis=-1, keepdims=True)
    e = jnp.exp(scores - top)
    return (e * (1.0 / jnp.sum(e, axis=-1, keepdims=True))).astype(BF16)


def row_logits(rows, x_ref, lens_ref, w_ref, part_ref, v_ref):
    n, width = x_ref.shape
    length = n // rows
    packed = dot(normalize(x_ref[...]), w_ref[...]).astype(BF16)
    v_ref[...] = packed[:, 2 * width :]
    place = place_of()
    lens = lens_ref[...]
    keeps = [iota((length, 1), 0) < row_length(lens, place * rows + r) for r in range(rows)]
    for pair in range(H // 2):
        lo = pair * 2 * HD
        q = [packed[r * length : (r + 1) * length, lo : lo + 2 * HD] for r in range(rows)]
        k = [packed[r * length : (r + 1) * length, width + lo : width + lo + 2 * HD] for r in range(rows)]
        k = [jnp.where(keep, part, jnp.zeros_like(part)) for keep, part in zip(keeps, k)]
        wide_q = jnp.concatenate([two_heads(part) for part in q], axis=1)
        wide_k = jnp.concatenate(k, axis=1)
        share = dot_t(wide_q, wide_k)
        part_ref[pair * 2 * length : (pair + 1) * 2 * length, :] = share.astype(part_ref.dtype)


def sum_shares(scale, got_ref, out_ref):
    total = jnp.sum(got_ref[...].astype(F32), axis=0) * scale
    level = jnp.max(total[:, :SHORTEST], axis=1, keepdims=True)
    total = (total - level).astype(out_ref.dtype)
    out_ref[...] = jnp.broadcast_to(total[None], out_ref.shape)


def row_mix(rows, tied_ref, v_ref, x_ref, lens_ref, w_ref, out_ref, mixed_ref):
    n, width = x_ref.shape
    length = n // rows
    place = place_of()
    lens = lens_ref[...]
    for r in range(rows):
        keep = iota((1, length), 1) < row_length(lens, place * rows + r)
        for pair in range(H // 2):
            lo = pair * 2 * HD
            tied = tied_ref[pair * 2 * length : (pair + 1) * 2 * length, :].astype(F32)
            p = soft(jnp.where(keep, tied, NEG))
            both = dot(p, v_ref[r * length : (r + 1) * length, lo : lo + 2 * HD])
            mixed_ref[r * length : (r + 1) * length, lo : lo + 2 * HD] = pick_heads(both).astype(BF16)
    after = (x_ref[...].astype(F32) + dot(mixed_ref[...], w_ref[...])).astype(BF16)
    here, there = iota((n, n), 0), iota((n, n), 1)
    order = (there == (here % rows) * length + here // rows).astype(BF16)
    out_ref[...] = dot(order, after).astype(BF16)


def column_block(rows, x_ref, lens_ref, wqkv_ref, wout_ref, out_ref, mixed_ref):
    n, width = x_ref.shape
    all_rows = lens_ref.shape[1]
    devices = all_rows // rows
    chunk = n // devices
    columns = chunk // rows
    x = x_ref[...]
    packed = dot(normalize(x), wqkv_ref[...]).astype(BF16)
    token = iota((all_rows, n), 1)
    row_of = token // chunk * rows + token % rows
    spread_rows = (row_of == iota((all_rows, n), 0)).astype(BF16)
    lens = jnp.broadcast_to(lens_ref[...].astype(F32), (8, all_rows)).astype(BF16)
    token_lens = dot(lens, spread_rows)[0:1]
    residue_k = iota((n, n), 1) % chunk // rows
    residue_q = iota((n, n), 0) % chunk // rows
    inside = (place_of() * columns + iota((1, n), 1) % chunk // rows).astype(F32) < token_lens
    bias = jnp.where((residue_k == residue_q) & inside, 0.0, NEG)
    bias = jnp.concatenate([bias, bias], axis=0)
    for pair in range(H // 2):
        lo = pair * 2 * HD
        q = two_heads(packed[:, lo : lo + 2 * HD])
        scores = dot_t(q, packed[:, width + lo : width + lo + 2 * HD]) * (1.0 / math.sqrt(HD)) + bias
        both = dot(soft(scores), packed[:, 2 * width + lo : 2 * width + lo + 2 * HD])
        mixed_ref[:, lo : lo + 2 * HD] = pick_heads(both).astype(BF16)
    out_ref[...] = (x.astype(F32) + dot(mixed_ref[...], wout_ref[...])).astype(BF16)


def finish(rows, y_ref, tokens_ref, embed_ref, out_ref):
    n, _ = y_ref.shape
    length = n // rows
    here, there = iota((n, n), 0), iota((n, n), 1)
    order = (there == (here % length) * rows + here // length).astype(BF16)
    handed = dot(order, y_ref[...])
    first = (lax.axis_index("section") == 0).astype(F32)
    table = embed_ref[...]
    for r in range(rows):
        onehot = (iota((table.shape[0], length), 0) == tokens_ref[r : r + 1, :]).astype(F32) * first
        looked = lax.dot_general(
            onehot.astype(BF16), table, (((0,), (0,)), ((), ())), preferred_element_type=F32
        )
        out_ref[r * length : (r + 1) * length, :] = (handed[r * length : (r + 1) * length] + looked).astype(BF16)


def call(body, name, shapes, *operands, scratch=()):
    vmem = pl.BlockSpec(memory_space=pltpu.VMEM)
    return pl.pallas_call(
        body,
        out_shape=shapes,
        in_specs=[vmem] * len(operands),
        out_specs=jax.tree.map(lambda _: vmem, shapes),
        scratch_shapes=list(scratch),
        compiler_params=pltpu.CompilerParams(vmem_limit_bytes=40 * 1024 * 1024),
        name=name,
    )(*operands)


def exchange(blocks):
    return lax.all_to_all(blocks, GROUP, split_axis=0, concat_axis=0, tiled=True)


def local(slab, tokens, lengths, embed, row_qkv, row_out, col_qkv, col_out):
    _, rows, length, width = slab.shape
    all_rows = lengths.shape[1]
    devices = all_rows // rows
    n = rows * length
    piece = H * length // devices
    sds = jax.ShapeDtypeStruct
    x = slab.reshape(n, width)
    shares, values = call(
        functools.partial(row_logits, rows),
        "row_logits",
        (sds((H * length, length), BF16), sds((n, width), BF16)),
        x,
        lengths,
        row_qkv[0],
    )
    got = exchange(shares.reshape(devices, piece, length))
    summed = call(
        functools.partial(sum_shares, 1.0 / math.sqrt(HD * all_rows)),
        "sum_shares",
        sds((devices, piece, length), BF16),
        got,
    )
    tied = exchange(summed).reshape(H * length, length)
    mixed = pltpu.VMEM((n, width), BF16)
    after = call(
        functools.partial(row_mix, rows),
        "row_mix",
        sds((n, width), BF16),
        tied,
        values,
        x,
        lengths,
        row_out[0],
        scratch=[mixed],
    )
    regrouped = exchange(after.reshape(devices, n // devices, width)).reshape(n, width)
    y = call(
        functools.partial(column_block, rows),
        "column_block",
        sds((n, width), BF16),
        regrouped,
        lengths,
        col_qkv[0],
        col_out[0],
        scratch=[mixed],
    )
    sections = lax.axis_size("section")
    handed = lax.ppermute(y, "section", [(s, s + 1) for s in range(sections - 1)])
    restored = exchange(handed.reshape(devices, n // devices, width)).reshape(n, width)
    out = call(
        functools.partial(finish, rows),
        "finish",
        sds((n, width), BF16),
        restored,
        tokens,
        embed,
    )
    return out.reshape(slab.shape)


def solution(mesh):
    in_specs = (
        P("section", ("depth", "res"), None, None),
        P(("depth", "res"), None),
        P("section", None),
        P(),
        P("section", None, None),
        P("section", None, None),
        P("section", None, None),
        P("section", None, None),
    )
    out_specs = P("section", ("depth", "res"), None, None)
    return jax.shard_map(local, mesh=mesh, in_specs=in_specs, out_specs=out_specs, check_vma=False)
```

```python
import functools
import math

import jax
import jax.numpy as jnp
from jax import lax
from jax.experimental import pallas as pl
from jax.experimental.pallas import tpu as pltpu
from jax.sharding import PartitionSpec as P

H = 12
HD = 64
GROUP = ("depth", "res")
SHORTEST = 24
DELAY = 3000
ALL_VMEM = 67_043_328
ROOM = 20_000_000
ROOM_LOGITS = 3_000_000
COVER = 4_000_000_000
NEG = -1e30
F32 = jnp.float32
BF16 = jnp.bfloat16


def iota(shape, dim):
    return lax.broadcasted_iota(jnp.int32, shape, dim)


def dot(a, b):
    return jnp.dot(a, b, preferred_element_type=F32)


def dot_t(a, b):
    return lax.dot_general(a, b, (((1,), (1,)), ((), ())), preferred_element_type=F32)


def normalize(values):
    values = values.astype(F32)
    center = jnp.mean(values, axis=-1, keepdims=True)
    off = values - center
    spread = jnp.mean(off * off, axis=-1, keepdims=True)
    return (off * lax.rsqrt(spread + 1e-05)).astype(BF16)


def place_of():
    return lax.axis_index(GROUP)


def two_heads(tile):
    first = iota(tile.shape, 1) < HD
    none = jnp.zeros_like(tile)
    return jnp.concatenate([jnp.where(first, tile, none), jnp.where(first, none, tile)], axis=0)


def pick_heads(both):
    n = both.shape[0] // 2
    return jnp.where(iota((n, 2 * HD), 1) < HD, both[:n], both[n:])


def soft(scores):
    top = jnp.max(scores, axis=-1, keepdims=True)
    e = jnp.exp(scores - top)
    return (e * (1.0 / jnp.sum(e, axis=-1, keepdims=True))).astype(BF16)


def pack(block):
    m = block.shape[0] // 2
    third = block.shape[0] // 3
    left, right = block[:, :HD], block[:, HD:]
    wide = jnp.concatenate([left[:m], left[m:]], axis=1)
    rest = [right[i * third : (i + 1) * third] for i in range(3)]
    rest = jnp.concatenate(rest + [jnp.zeros_like(rest[0])], axis=1)
    return jnp.concatenate([wide, rest], axis=0)


def unpack(block):
    m = block.shape[0] * 3 // 5
    wide, rest = block[:m], block[m:]
    left = jnp.concatenate([wide[:, :HD], wide[:, HD:]], axis=0)
    right = jnp.concatenate([rest[:, :32], rest[:, 32:64], rest[:, 64:96]], axis=0)
    return jnp.concatenate([left, right], axis=1)


def own_lengths(lens, rows):
    row = lax.axis_index(GROUP) * rows + iota((rows, lens.shape[1]), 0)
    return jnp.sum(jnp.where(iota(row.shape, 1) == row, lens, 0), axis=1, keepdims=True)


def row_logits(rows, x_hbm, lens_hbm, w_hbm, part_ref, v_ref, x_ref, lens_ref, w_ref, sems):
    n, width = x_hbm.shape
    length = n // rows
    parts = w_ref.shape[0]
    copies = [
        pltpu.make_async_copy(w_hbm.at[:, pl.ds(i * width, width)], w_ref.at[i], sems.at[i])
        for i in range(parts)
    ]
    copy_x = pltpu.make_async_copy(x_hbm, x_ref, sems.at[parts])
    copy_lens = pltpu.make_async_copy(lens_hbm, lens_ref, sems.at[parts + 1])
    for copy in [copy_x, copy_lens] + copies:
        copy.start()

    @pl.when(lax.axis_index("section") % 2 == 0)
    def _():
        pl.delay(DELAY)

    copy_lens.wait()
    mine = own_lengths(lens_ref[...], rows)
    copy_x.wait()
    normed = normalize(x_ref[...])
    packed = []
    for i, copy in enumerate(copies[:2]):
        copy.wait()
        packed.append(dot(normed, w_ref[i]).astype(BF16))
    packed = jnp.concatenate(packed, axis=1)
    keeps = [iota((length, 1), 0) < mine[r : r + 1] for r in range(rows)]
    for pair in range(H // 2):
        lo = pair * 2 * HD
        q = [packed[r * length : (r + 1) * length, lo : lo + 2 * HD] for r in range(rows)]
        k = [packed[r * length : (r + 1) * length, width + lo : width + lo + 2 * HD] for r in range(rows)]
        k = [jnp.where(keep, part, jnp.zeros_like(part)) for keep, part in zip(keeps, k)]
        wide_q = jnp.concatenate([two_heads(part) for part in q], axis=1)
        wide_k = jnp.concatenate(k, axis=1)
        share = dot_t(wide_q, wide_k)
        half = length // 2
        for i in range(4):
            part_ref[pair * 4 + i] = pack(share[i * half : (i + 1) * half]).astype(part_ref.dtype)
    copies[2].wait()
    v_ref[...] = dot(normed, w_ref[2]).astype(BF16)


def sum_shares(scale, got_ref, out_ref):
    total = unpack(jnp.sum(got_ref[...].astype(F32), axis=0) * scale)
    level = jnp.max(total[:, :SHORTEST], axis=1, keepdims=True)
    total = pack(total - level).astype(out_ref.dtype)
    out_ref[...] = jnp.broadcast_to(total[None], out_ref.shape)


def row_mix(rows, tied_ref, v_ref, x_ref, lens_ref, wout_ref, out_ref, mixed_ref):
    n, width = x_ref.shape
    length = n // rows
    mine = own_lengths(lens_ref[...], rows)
    tied = [
        jnp.concatenate([unpack(tied_ref[pair * 4 + i].astype(F32)) for i in range(4)], axis=0)
        for pair in range(H // 2)
    ]
    for r in range(rows):
        keep = iota((1, length), 1) < mine[r : r + 1]
        for pair in range(H // 2):
            lo = pair * 2 * HD
            p = soft(jnp.where(keep, tied[pair], NEG))
            both = dot(p, v_ref[r * length : (r + 1) * length, lo : lo + 2 * HD])
            mixed_ref[r * length : (r + 1) * length, lo : lo + 2 * HD] = pick_heads(both).astype(BF16)
    after = (x_ref[...].astype(F32) + dot(mixed_ref[...], wout_ref[...])).astype(BF16)
    here, there = iota((n, n), 0), iota((n, n), 1)
    order = (there == (here % rows) * length + here // rows).astype(BF16)
    out_ref[...] = dot(order, after).astype(BF16)


def column_block(rows, x_ref, lens_ref, wqkv_ref, wout_ref, out_ref, mixed_ref):
    n, width = x_ref.shape
    all_rows = lens_ref.shape[1]
    devices = all_rows // rows
    chunk = n // devices
    columns = chunk // rows
    x = x_ref[...]
    packed = dot(normalize(x), wqkv_ref[...]).astype(BF16)
    token = iota((all_rows, n), 1)
    row_of = token // chunk * rows + token % rows
    spread_rows = (row_of == iota((all_rows, n), 0)).astype(BF16)
    lens = jnp.broadcast_to(lens_ref[...].astype(F32), (8, all_rows)).astype(BF16)
    token_lens = dot(lens, spread_rows)[0:1]
    residue_k = iota((n, n), 1) % chunk // rows
    residue_q = iota((n, n), 0) % chunk // rows
    inside = (place_of() * columns + iota((1, n), 1) % chunk // rows).astype(F32) < token_lens
    bias = jnp.where((residue_k == residue_q) & inside, 0.0, NEG)
    bias = jnp.concatenate([bias, bias], axis=0)
    for pair in range(H // 2):
        lo = pair * 2 * HD
        q = two_heads(packed[:, lo : lo + 2 * HD])
        scores = dot_t(q, packed[:, width + lo : width + lo + 2 * HD]) * (1.0 / math.sqrt(HD)) + bias
        both = dot(soft(scores), packed[:, 2 * width + lo : 2 * width + lo + 2 * HD])
        mixed_ref[:, lo : lo + 2 * HD] = pick_heads(both).astype(BF16)
    out_ref[...] = (x.astype(F32) + dot(mixed_ref[...], wout_ref[...])).astype(BF16)


def finish(rows, y_ref, tokens_ref, embed_ref, out_ref):
    n, _ = y_ref.shape
    length = n // rows
    last = lax.axis_index("section") == lax.axis_size("section") - 1

    @pl.when(jnp.logical_not(last))
    def _():
        here, there = iota((n, n), 0), iota((n, n), 1)
        order = (there == (here % length) * rows + here // length).astype(BF16)
        out_ref[...] = dot(order, y_ref[...]).astype(BF16)

    @pl.when(last)
    def _():
        table = embed_ref[...]
        for r in range(rows):
            onehot = (iota((table.shape[0], length), 0) == tokens_ref[r : r + 1, :]).astype(BF16)
            looked = lax.dot_general(
                onehot, table, (((0,), (0,)), ((), ())), preferred_element_type=F32
            )
            out_ref[r * length : (r + 1) * length, :] = looked.astype(BF16)


def call(body, name, shapes, *operands, scratch=(), far=(), room=ROOM, cost=None):
    vmem = pl.BlockSpec(memory_space=pltpu.VMEM)
    hbm = pl.BlockSpec(memory_space=pltpu.HBM)
    return pl.pallas_call(
        body,
        out_shape=shapes,
        in_specs=[hbm if i in far else vmem for i in range(len(operands))],
        out_specs=jax.tree.map(lambda _: vmem, shapes),
        scratch_shapes=list(scratch),
        compiler_params=pltpu.CompilerParams(vmem_limit_bytes=ALL_VMEM - room),
        cost_estimate=cost,
        name=name,
    )(*operands)


def exchange(blocks):
    return lax.all_to_all(blocks, GROUP, split_axis=0, concat_axis=0, tiled=True)


def local(slab, tokens, lengths, embed, row_qkv, row_out, col_qkv, col_out):
    _, rows, length, width = slab.shape
    all_rows = lengths.shape[1]
    devices = all_rows // rows
    n = rows * length
    piece = length // 4 + 16
    sds = jax.ShapeDtypeStruct
    x = slab.reshape(n, width)
    shares, values = call(
        functools.partial(row_logits, rows),
        "row_logits",
        (sds((devices, piece, 2 * HD), BF16), sds((n, width), BF16)),
        x,
        lengths,
        row_qkv[0],
        far=(0, 1, 2),
        room=ROOM_LOGITS,
        scratch=[
            pltpu.VMEM((n, width), BF16),
            pltpu.VMEM(lengths.shape, jnp.int32),
            pltpu.VMEM((3, width, width), BF16),
            pltpu.SemaphoreType.DMA((5,)),
        ],
    )
    got = exchange(shares)
    summed = call(
        functools.partial(sum_shares, 1.0 / math.sqrt(HD * all_rows)),
        "sum_shares",
        sds((devices, piece, 2 * HD), BF16),
        got,
        cost=pl.CostEstimate(flops=COVER, bytes_accessed=0, transcendentals=0),
    )
    tied = exchange(summed)
    mixed = pltpu.VMEM((n, width), BF16)
    after = call(
        functools.partial(row_mix, rows),
        "row_mix",
        sds((n, width), BF16),
        tied,
        values,
        x,
        lengths,
        row_out[0],
        scratch=[mixed],
    )
    regrouped = exchange(after.reshape(devices, n // devices, width)).reshape(n, width)
    y = call(
        functools.partial(column_block, rows),
        "column_block",
        sds((n, width), BF16),
        regrouped,
        lengths,
        col_qkv[0],
        col_out[0],
        scratch=[mixed],
    )
    restored = exchange(y.reshape(devices, n // devices, width)).reshape(n, width)
    out = call(
        functools.partial(finish, rows),
        "finish",
        sds((n, width), BF16),
        restored,
        tokens,
        embed,
    )
    sections = lax.axis_size("section")
    out = lax.ppermute(out, "section", [(s, (s + 1) % sections) for s in range(sections)])
    return out.reshape(slab.shape)


def solution(mesh):
    in_specs = (
        P("section", ("depth", "res"), None, None),
        P(("depth", "res"), None),
        P("section", None),
        P(),
        P("section", None, None),
        P("section", None, None),
        P("section", None, None),
        P("section", None, None),
    )
    out_specs = P("section", ("depth", "res"), None, None)
    return jax.shard_map(local, mesh=mesh, in_specs=in_specs, out_specs=out_specs, check_vma=False)
```

```python
import functools
import math

import jax
import jax.numpy as jnp
from jax import lax
from jax.experimental import pallas as pl
from jax.experimental.pallas import tpu as pltpu
from jax.sharding import PartitionSpec as P

H = 12
HD = 64
GROUP = ("depth", "res")
SHORTEST = 24
DELAY = 3000
ALL_VMEM = 67_043_328
ROOM = 20_000_000
ROOM_LOGITS = 3_000_000
COVER = 4_000_000_000
NEG = -1e30
F32 = jnp.float32
BF16 = jnp.bfloat16


def iota(shape, dim):
    return lax.broadcasted_iota(jnp.int32, shape, dim)


def dot(a, b):
    return jnp.dot(a, b, preferred_element_type=F32)


def dot_t(a, b):
    return lax.dot_general(a, b, (((1,), (1,)), ((), ())), preferred_element_type=F32)


def normalize(values):
    values = values.astype(F32)
    center = jnp.mean(values, axis=-1, keepdims=True)
    off = values - center
    spread = jnp.mean(off * off, axis=-1, keepdims=True)
    return (off * lax.rsqrt(spread + 1e-05)).astype(BF16)


def place_of():
    return lax.axis_index(GROUP)


def two_heads(tile):
    first = iota(tile.shape, 1) < HD
    none = jnp.zeros_like(tile)
    return jnp.concatenate([jnp.where(first, tile, none), jnp.where(first, none, tile)], axis=0)


def pick_heads(both):
    n = both.shape[0] // 2
    return jnp.where(iota((n, 2 * HD), 1) < HD, both[:n], both[n:])


def soft(scores):
    top = jnp.max(scores, axis=-1, keepdims=True)
    e = jnp.exp(scores - top)
    return (e * (1.0 / jnp.sum(e, axis=-1, keepdims=True))).astype(BF16)


def attend(scores, values):
    weights = jnp.exp(scores - jnp.max(scores, axis=-1, keepdims=True)).astype(BF16)
    width = values.shape[1]
    both = dot(weights, jnp.concatenate([values, jnp.ones_like(values)], axis=1))
    return both[:, :width] * (1.0 / both[:, width:])


def pack(block):
    m = block.shape[0] // 2
    third = block.shape[0] // 3
    left, right = block[:, :HD], block[:, HD:]
    wide = jnp.concatenate([left[:m], left[m:]], axis=1)
    rest = [right[i * third : (i + 1) * third] for i in range(3)]
    rest = jnp.concatenate(rest + [jnp.zeros_like(rest[0])], axis=1)
    return jnp.concatenate([wide, rest], axis=0)


def unpack(block):
    m = block.shape[0] * 3 // 5
    wide, rest = block[:m], block[m:]
    left = jnp.concatenate([wide[:, :HD], wide[:, HD:]], axis=0)
    right = jnp.concatenate([rest[:, :32], rest[:, 32:64], rest[:, 64:96]], axis=0)
    return jnp.concatenate([left, right], axis=1)


def own_lengths(lens, rows):
    row = lax.axis_index(GROUP) * rows + iota((rows, lens.shape[1]), 0)
    return jnp.sum(jnp.where(iota(row.shape, 1) == row, lens, 0), axis=1, keepdims=True)


def row_logits(rows, x_hbm, lens_hbm, w_hbm, part_ref, v_ref, x_ref, lens_ref, w_ref, sems):
    n, width = x_hbm.shape
    length = n // rows
    parts = w_ref.shape[0]
    copies = [
        pltpu.make_async_copy(w_hbm.at[:, pl.ds(i * width, width)], w_ref.at[i], sems.at[i])
        for i in range(parts)
    ]
    copy_x = pltpu.make_async_copy(x_hbm, x_ref, sems.at[parts])
    copy_lens = pltpu.make_async_copy(lens_hbm, lens_ref, sems.at[parts + 1])
    for copy in [copy_x, copy_lens] + copies:
        copy.start()

    @pl.when(lax.axis_index("section") % 2 == 0)
    def _():
        pl.delay(DELAY)

    copy_lens.wait()
    mine = own_lengths(lens_ref[...], rows)
    copy_x.wait()
    normed = normalize(x_ref[...])
    packed = []
    for i, copy in enumerate(copies[:2]):
        copy.wait()
        packed.append(dot(normed, w_ref[i]).astype(BF16))
    packed = jnp.concatenate(packed, axis=1)
    keeps = [iota((length, 1), 0) < mine[r : r + 1] for r in range(rows)]
    for pair in range(H // 2):
        lo = pair * 2 * HD
        q = [packed[r * length : (r + 1) * length, lo : lo + 2 * HD] for r in range(rows)]
        k = [packed[r * length : (r + 1) * length, width + lo : width + lo + 2 * HD] for r in range(rows)]
        k = [jnp.where(keep, part, jnp.zeros_like(part)) for keep, part in zip(keeps, k)]
        wide_q = jnp.concatenate([two_heads(part) for part in q], axis=1)
        wide_k = jnp.concatenate(k, axis=1)
        share = dot_t(wide_q, wide_k)
        half = length // 2
        for i in range(4):
            part_ref[pair * 4 + i] = pack(share[i * half : (i + 1) * half]).astype(part_ref.dtype)
    copies[2].wait()
    v_ref[...] = dot(normed, w_ref[2]).astype(BF16)


def sum_shares(scale, got_ref, out_ref):
    total = unpack(jnp.sum(got_ref[...].astype(F32), axis=0) * scale)
    level = jnp.max(total[:, :SHORTEST], axis=1, keepdims=True)
    total = pack(total - level).astype(out_ref.dtype)
    out_ref[...] = jnp.broadcast_to(total[None], out_ref.shape)


def row_mix(rows, tied_ref, v_ref, x_ref, lens_ref, wout_ref, out_ref, mixed_ref):
    n, width = x_ref.shape
    length = n // rows
    mine = own_lengths(lens_ref[...], rows)
    tied = [
        jnp.concatenate([unpack(tied_ref[pair * 4 + i].astype(F32)) for i in range(4)], axis=0)
        for pair in range(H // 2)
    ]
    for r in range(rows):
        keep = iota((1, length), 1) < mine[r : r + 1]
        for pair in range(H // 2):
            lo = pair * 2 * HD
            p = soft(jnp.where(keep, tied[pair], NEG))
            both = dot(p, v_ref[r * length : (r + 1) * length, lo : lo + 2 * HD])
            mixed_ref[r * length : (r + 1) * length, lo : lo + 2 * HD] = pick_heads(both).astype(BF16)
    after = (x_ref[...].astype(F32) + dot(mixed_ref[...], wout_ref[...])).astype(BF16)
    here, there = iota((n, n), 0), iota((n, n), 1)
    order = (there == (here % rows) * length + here // rows).astype(BF16)
    out_ref[...] = dot(order, after).astype(BF16)


def column_block(rows, x_ref, lens_ref, wqkv_ref, wout_ref, out_ref, mixed_ref):
    n, width = x_ref.shape
    all_rows = lens_ref.shape[1]
    devices = all_rows // rows
    chunk = n // devices
    columns = chunk // rows
    x = x_ref[...]
    packed = dot(normalize(x), wqkv_ref[...]).astype(BF16)
    token = iota((all_rows, n), 1)
    row_of = token // chunk * rows + token % rows
    spread_rows = (row_of == iota((all_rows, n), 0)).astype(BF16)
    lens = jnp.broadcast_to(lens_ref[...].astype(F32), (8, all_rows)).astype(BF16)
    token_lens = dot(lens, spread_rows)[0:1]
    residue_k = iota((n, n), 1) % chunk // rows
    residue_q = iota((n, n), 0) % chunk // rows
    inside = (place_of() * columns + iota((1, n), 1) % chunk // rows).astype(F32) < token_lens
    bias = jnp.where((residue_k == residue_q) & inside, 0.0, NEG)
    bias = jnp.concatenate([bias, bias], axis=0)
    for pair in range(H // 2):
        lo = pair * 2 * HD
        q = two_heads(packed[:, lo : lo + 2 * HD] * jnp.asarray(1.0 / math.sqrt(HD), BF16))
        scores = dot_t(q, packed[:, width + lo : width + lo + 2 * HD]) + bias
        both = attend(scores, packed[:, 2 * width + lo : 2 * width + lo + 2 * HD])
        mixed_ref[:, lo : lo + 2 * HD] = pick_heads(both).astype(BF16)
    out_ref[...] = (x.astype(F32) + dot(mixed_ref[...], wout_ref[...])).astype(BF16)


def finish(rows, y_ref, tokens_ref, embed_ref, out_ref):
    n, _ = y_ref.shape
    length = n // rows
    last = lax.axis_index("section") == lax.axis_size("section") - 1

    @pl.when(jnp.logical_not(last))
    def _():
        here, there = iota((n, n), 0), iota((n, n), 1)
        order = (there == (here % length) * rows + here // length).astype(BF16)
        out_ref[...] = dot(order, y_ref[...]).astype(BF16)

    @pl.when(last)
    def _():
        table = embed_ref[...]
        for r in range(rows):
            onehot = (iota((table.shape[0], length), 0) == tokens_ref[r : r + 1, :]).astype(BF16)
            looked = lax.dot_general(
                onehot, table, (((0,), (0,)), ((), ())), preferred_element_type=F32
            )
            out_ref[r * length : (r + 1) * length, :] = looked.astype(BF16)


def call(body, name, shapes, *operands, scratch=(), far=(), room=ROOM, cost=None):
    vmem = pl.BlockSpec(memory_space=pltpu.VMEM)
    hbm = pl.BlockSpec(memory_space=pltpu.HBM)
    return pl.pallas_call(
        body,
        out_shape=shapes,
        in_specs=[hbm if i in far else vmem for i in range(len(operands))],
        out_specs=jax.tree.map(lambda _: vmem, shapes),
        scratch_shapes=list(scratch),
        compiler_params=pltpu.CompilerParams(vmem_limit_bytes=ALL_VMEM - room),
        cost_estimate=cost,
        name=name,
    )(*operands)


def exchange(blocks):
    return lax.all_to_all(blocks, GROUP, split_axis=0, concat_axis=0, tiled=True)


def local(slab, tokens, lengths, embed, row_qkv, row_out, col_qkv, col_out):
    _, rows, length, width = slab.shape
    all_rows = lengths.shape[1]
    devices = all_rows // rows
    n = rows * length
    piece = length // 4 + 16
    sds = jax.ShapeDtypeStruct
    x = slab.reshape(n, width)
    shares, values = call(
        functools.partial(row_logits, rows),
        "row_logits",
        (sds((devices, piece, 2 * HD), BF16), sds((n, width), BF16)),
        x,
        lengths,
        row_qkv[0],
        far=(0, 1, 2),
        room=ROOM_LOGITS,
        scratch=[
            pltpu.VMEM((n, width), BF16),
            pltpu.VMEM(lengths.shape, jnp.int32),
            pltpu.VMEM((3, width, width), BF16),
            pltpu.SemaphoreType.DMA((5,)),
        ],
    )
    got = exchange(shares)
    summed = call(
        functools.partial(sum_shares, 1.0 / math.sqrt(HD * all_rows)),
        "sum_shares",
        sds((devices, piece, 2 * HD), BF16),
        got,
        cost=pl.CostEstimate(flops=COVER, bytes_accessed=0, transcendentals=0),
    )
    tied = exchange(summed)
    mixed = pltpu.VMEM((n, width), BF16)
    after = call(
        functools.partial(row_mix, rows),
        "row_mix",
        sds((n, width), BF16),
        tied,
        values,
        x,
        lengths,
        row_out[0],
        scratch=[mixed],
    )
    regrouped = exchange(after.reshape(devices, n // devices, width)).reshape(n, width)
    y = call(
        functools.partial(column_block, rows),
        "column_block",
        sds((n, width), BF16),
        regrouped,
        lengths,
        col_qkv[0],
        col_out[0],
        scratch=[mixed],
    )
    restored = exchange(y.reshape(devices, n // devices, width)).reshape(n, width)
    out = call(
        functools.partial(finish, rows),
        "finish",
        sds((n, width), BF16),
        restored,
        tokens,
        embed,
    )
    sections = lax.axis_size("section")
    out = lax.ppermute(out, "section", [(s, (s + 1) % sections) for s in range(sections)])
    return out.reshape(slab.shape)


def solution(mesh):
    in_specs = (
        P("section", ("depth", "res"), None, None),
        P(("depth", "res"), None),
        P("section", None),
        P(),
        P("section", None, None),
        P("section", None, None),
        P("section", None, None),
        P("section", None, None),
    )
    out_specs = P("section", ("depth", "res"), None, None)
    return jax.shard_map(local, mesh=mesh, in_specs=in_specs, out_specs=out_specs, check_vma=False)
```

```python
import functools
import math

import jax
import jax.numpy as jnp
from jax import lax
from jax.experimental import pallas as pl
from jax.experimental.pallas import tpu as pltpu
from jax.sharding import PartitionSpec as P

H = 12
HD = 64
GROUP = ("depth", "res")
SHORTEST = 24
DELAY = 3000
ALL_VMEM = 67_043_328
ROOM = 20_000_000
ROOM_LOGITS = 3_000_000
COVER = 4_000_000_000
NEG = -1e30
F32 = jnp.float32
BF16 = jnp.bfloat16


def iota(shape, dim):
    return lax.broadcasted_iota(jnp.int32, shape, dim)


def dot(a, b):
    return jnp.dot(a, b, preferred_element_type=F32)


def dot_t(a, b):
    return lax.dot_general(a, b, (((1,), (1,)), ((), ())), preferred_element_type=F32)


def normalize(values):
    values = values.astype(F32)
    center = jnp.mean(values, axis=-1, keepdims=True)
    off = values - center
    spread = jnp.mean(off * off, axis=-1, keepdims=True)
    return (off * lax.rsqrt(spread + 1e-05)).astype(BF16)


def turned(place, ring):
    back = 3 * ring - 1 - place
    return (place if place < ring else back) if isinstance(place, int) else jnp.where(place < ring, place, back)


def place_of():
    return lax.axis_index(GROUP)


def two_heads(tile):
    first = iota(tile.shape, 1) < HD
    none = jnp.zeros_like(tile)
    return jnp.concatenate([jnp.where(first, tile, none), jnp.where(first, none, tile)], axis=0)


def pick_heads(both):
    n = both.shape[0] // 2
    return jnp.where(iota((n, 2 * HD), 1) < HD, both[:n], both[n:])


def soft(scores):
    top = jnp.max(scores, axis=-1, keepdims=True)
    e = jnp.exp(scores - top)
    return (e * (1.0 / jnp.sum(e, axis=-1, keepdims=True))).astype(BF16)


def attend(scores, values):
    weights = jnp.exp(scores - jnp.max(scores, axis=-1, keepdims=True)).astype(BF16)
    width = values.shape[1]
    both = dot(weights, jnp.concatenate([values, jnp.ones_like(values)], axis=1))
    return both[:, :width] * (1.0 / both[:, width:])


def pack(block):
    m = block.shape[0] // 2
    third = block.shape[0] // 3
    left, right = block[:, :HD], block[:, HD:]
    wide = jnp.concatenate([left[:m], left[m:]], axis=1)
    rest = [right[i * third : (i + 1) * third] for i in range(3)]
    rest = jnp.concatenate(rest + [jnp.zeros_like(rest[0])], axis=1)
    return jnp.concatenate([wide, rest], axis=0)


def unpack(block):
    m = block.shape[0] * 3 // 5
    wide, rest = block[:m], block[m:]
    left = jnp.concatenate([wide[:, :HD], wide[:, HD:]], axis=0)
    right = jnp.concatenate([rest[:, :32], rest[:, 32:64], rest[:, 64:96]], axis=0)
    return jnp.concatenate([left, right], axis=1)


def own_lengths(lens, rows):
    row = lax.axis_index(GROUP) * rows + iota((rows, lens.shape[1]), 0)
    return jnp.sum(jnp.where(iota(row.shape, 1) == row, lens, 0), axis=1, keepdims=True)


def row_logits(rows, x_hbm, lens_hbm, w_hbm, part_ref, v_ref, x_ref, lens_ref, w_ref, sems):
    n, width = x_hbm.shape
    length = n // rows
    parts = w_ref.shape[0]
    copies = [
        pltpu.make_async_copy(w_hbm.at[:, pl.ds(i * width, width)], w_ref.at[i], sems.at[i])
        for i in range(parts)
    ]
    copy_x = pltpu.make_async_copy(x_hbm, x_ref, sems.at[parts])
    copy_lens = pltpu.make_async_copy(lens_hbm, lens_ref, sems.at[parts + 1])
    for copy in [copy_x, copy_lens] + copies:
        copy.start()

    @pl.when(lax.axis_index("section") % 2 == 0)
    def _():
        pl.delay(DELAY)

    copy_lens.wait()
    mine = own_lengths(lens_ref[...], rows)
    copy_x.wait()
    normed = normalize(x_ref[...])
    packed = []
    for i, copy in enumerate(copies[:2]):
        copy.wait()
        packed.append(dot(normed, w_ref[i]).astype(BF16))
    packed = jnp.concatenate(packed, axis=1)
    keeps = [iota((length, 1), 0) < mine[r : r + 1] for r in range(rows)]
    for pair in range(H // 2):
        lo = pair * 2 * HD
        q = [packed[r * length : (r + 1) * length, lo : lo + 2 * HD] for r in range(rows)]
        k = [packed[r * length : (r + 1) * length, width + lo : width + lo + 2 * HD] for r in range(rows)]
        k = [jnp.where(keep, part, jnp.zeros_like(part)) for keep, part in zip(keeps, k)]
        wide_q = jnp.concatenate([two_heads(part) for part in q], axis=1)
        wide_k = jnp.concatenate(k, axis=1)
        share = dot_t(wide_q, wide_k)
        half = length // 2
        for i in range(4):
            part_ref[pair * 4 + i] = pack(share[i * half : (i + 1) * half]).astype(part_ref.dtype)
    copies[2].wait()
    v_ref[...] = dot(normed, w_ref[2]).astype(BF16)


def sum_shares(scale, got_ref, out_ref):
    total = unpack(jnp.sum(got_ref[...].astype(F32), axis=0) * scale)
    level = jnp.max(total[:, :SHORTEST], axis=1, keepdims=True)
    total = pack(total - level).astype(out_ref.dtype)
    out_ref[...] = jnp.broadcast_to(total[None], out_ref.shape)


def row_mix(rows, tied_ref, v_ref, x_ref, lens_ref, wout_ref, out_ref, mixed_ref):
    n, width = x_ref.shape
    length = n // rows
    mine = own_lengths(lens_ref[...], rows)
    tied = [
        jnp.concatenate([unpack(tied_ref[pair * 4 + i].astype(F32)) for i in range(4)], axis=0)
        for pair in range(H // 2)
    ]
    for r in range(rows):
        keep = iota((1, length), 1) < mine[r : r + 1]
        for pair in range(H // 2):
            lo = pair * 2 * HD
            p = soft(jnp.where(keep, tied[pair], NEG))
            both = dot(p, v_ref[r * length : (r + 1) * length, lo : lo + 2 * HD])
            mixed_ref[r * length : (r + 1) * length, lo : lo + 2 * HD] = pick_heads(both).astype(BF16)
    after = (x_ref[...].astype(F32) + dot(mixed_ref[...], wout_ref[...])).astype(BF16)
    here, there = iota((n, n), 0), iota((n, n), 1)
    order = (there == (here % rows) * length + here // rows).astype(BF16)
    out_ref[...] = dot(order, after).astype(BF16)


def column_block(rows, x_ref, lens_ref, wqkv_ref, wout_ref, out_ref, mixed_ref):
    n, width = x_ref.shape
    all_rows = lens_ref.shape[1]
    devices = all_rows // rows
    chunk = n // devices
    columns = chunk // rows
    x = x_ref[...]
    packed = dot(normalize(x), wqkv_ref[...]).astype(BF16)
    token = iota((all_rows, n), 1)
    ring = devices // 2
    row_of = turned(token // chunk, ring) * rows + token % rows
    spread_rows = (row_of == iota((all_rows, n), 0)).astype(BF16)
    lens = jnp.broadcast_to(lens_ref[...].astype(F32), (8, all_rows)).astype(BF16)
    token_lens = dot(lens, spread_rows)[0:1]
    residue_k = iota((n, n), 1) % chunk // rows
    residue_q = iota((n, n), 0) % chunk // rows
    inside = (turned(place_of(), ring) * columns + iota((1, n), 1) % chunk // rows).astype(F32) < token_lens
    bias = jnp.where((residue_k == residue_q) & inside, 0.0, NEG)
    bias = jnp.concatenate([bias, bias], axis=0)
    for pair in range(H // 2):
        lo = pair * 2 * HD
        q = two_heads(packed[:, lo : lo + 2 * HD] * jnp.asarray(1.0 / math.sqrt(HD), BF16))
        scores = dot_t(q, packed[:, width + lo : width + lo + 2 * HD]) + bias
        both = attend(scores, packed[:, 2 * width + lo : 2 * width + lo + 2 * HD])
        mixed_ref[:, lo : lo + 2 * HD] = pick_heads(both).astype(BF16)
    out_ref[...] = (x.astype(F32) + dot(mixed_ref[...], wout_ref[...])).astype(BF16)


def finish(rows, y_ref, tokens_ref, embed_ref, out_ref):
    n, _ = y_ref.shape
    length = n // rows
    last = lax.axis_index("section") == lax.axis_size("section") - 1

    @pl.when(jnp.logical_not(last))
    def _():
        here, there = iota((n, n), 0), iota((n, n), 1)
        order = (there == (here % length) * rows + here // length).astype(BF16)
        out_ref[...] = dot(order, y_ref[...]).astype(BF16)

    @pl.when(last)
    def _():
        table = embed_ref[...]
        for r in range(rows):
            onehot = (iota((table.shape[0], length), 0) == tokens_ref[r : r + 1, :]).astype(BF16)
            looked = lax.dot_general(
                onehot, table, (((0,), (0,)), ((), ())), preferred_element_type=F32
            )
            out_ref[r * length : (r + 1) * length, :] = looked.astype(BF16)


def call(body, name, shapes, *operands, scratch=(), far=(), room=ROOM, cost=None):
    vmem = pl.BlockSpec(memory_space=pltpu.VMEM)
    hbm = pl.BlockSpec(memory_space=pltpu.HBM)
    return pl.pallas_call(
        body,
        out_shape=shapes,
        in_specs=[hbm if i in far else vmem for i in range(len(operands))],
        out_specs=jax.tree.map(lambda _: vmem, shapes),
        scratch_shapes=list(scratch),
        compiler_params=pltpu.CompilerParams(vmem_limit_bytes=ALL_VMEM - room),
        cost_estimate=cost,
        name=name,
    )(*operands)


def exchange(blocks):
    order = [turned(i, lax.axis_size("res")) for i in range(blocks.shape[0])]
    return lax.all_to_all(
        blocks, GROUP, split_axis=0, concat_axis=0, tiled=True, axis_index_groups=[order]
    )


def local(slab, tokens, lengths, embed, row_qkv, row_out, col_qkv, col_out):
    _, rows, length, width = slab.shape
    all_rows = lengths.shape[1]
    devices = all_rows // rows
    n = rows * length
    piece = length // 4 + 16
    sds = jax.ShapeDtypeStruct
    x = slab.reshape(n, width)
    shares, values = call(
        functools.partial(row_logits, rows),
        "row_logits",
        (sds((devices, piece, 2 * HD), BF16), sds((n, width), BF16)),
        x,
        lengths,
        row_qkv[0],
        far=(0, 1, 2),
        room=ROOM_LOGITS,
        scratch=[
            pltpu.VMEM((n, width), BF16),
            pltpu.VMEM(lengths.shape, jnp.int32),
            pltpu.VMEM((3, width, width), BF16),
            pltpu.SemaphoreType.DMA((5,)),
        ],
    )
    got = exchange(shares)
    summed = call(
        functools.partial(sum_shares, 1.0 / math.sqrt(HD * all_rows)),
        "sum_shares",
        sds((devices, piece, 2 * HD), BF16),
        got,
        cost=pl.CostEstimate(flops=COVER, bytes_accessed=0, transcendentals=0),
    )
    tied = exchange(summed)
    mixed = pltpu.VMEM((n, width), BF16)
    after = call(
        functools.partial(row_mix, rows),
        "row_mix",
        sds((n, width), BF16),
        tied,
        values,
        x,
        lengths,
        row_out[0],
        scratch=[mixed],
    )
    regrouped = exchange(after.reshape(devices, n // devices, width)).reshape(n, width)
    y = call(
        functools.partial(column_block, rows),
        "column_block",
        sds((n, width), BF16),
        regrouped,
        lengths,
        col_qkv[0],
        col_out[0],
        scratch=[mixed],
    )
    restored = exchange(y.reshape(devices, n // devices, width)).reshape(n, width)
    out = call(
        functools.partial(finish, rows),
        "finish",
        sds((n, width), BF16),
        restored,
        tokens,
        embed,
    )
    sections = lax.axis_size("section")
    out = lax.ppermute(out, "section", [(s, (s + 1) % sections) for s in range(sections)])
    return out.reshape(slab.shape)


def solution(mesh):
    in_specs = (
        P("section", ("depth", "res"), None, None),
        P(("depth", "res"), None),
        P("section", None),
        P(),
        P("section", None, None),
        P("section", None, None),
        P("section", None, None),
        P("section", None, None),
    )
    out_specs = P("section", ("depth", "res"), None, None)
    return jax.shard_map(local, mesh=mesh, in_specs=in_specs, out_specs=out_specs, check_vma=False)
```
